32 devices in a mesh: groups: 2 (over y), cell: 4 (over z), wall: 4 (over x, core).
Axes of the slice: x: 2, y: 2, z: 4, core: 2. Of those that a mesh axis runs over, the one named last changes fastest.
Arguments:
- mem_pos: float32 [3, 2048], P(None, ('groups', 'cell')), parts along dimension 1, may hold values from -0.7 to 8, as said below
- forces: bfloat16 [32, 3, 2048], P(None, None, ('groups', 'cell', 'wall')), parts along dimension 2, may hold values from -1.59375 to 1.59375
- wall_pos: float32 [3, 1024], P(None, ('groups', 'wall')), parts along dimension 1, may hold values from -1 to 8, as said below
- wall_normal: float32 [3, 1024], P(None, ('groups', 'wall')), parts along dimension 1, as said below
- wall_data: float32 [32, 3, 1024], P(None, None, ('groups', 'wall')), parts along dimension 2, may hold values from -6 to 6
- lag_density: bfloat16 [16, 3, 1024], P(None, None, ('groups', 'wall', 'cell')), parts along dimension 2, may hold values from -15 to 15
- batch_order: int32 [32], replicated, may hold values from 0 to 31, each once
Outputs:
- membrane_velocity: float32 [32, 3, 2048], P(None, None, ('groups', 'cell', 'wall')), parts along dimension 2
- wall_density: float32 [16, 3, 1024], P(None, None, ('groups', 'wall', 'cell')), parts along dimension 2
The draws below stay inside these ranges and needn't reach their ends.
There are 2 independent parts, one for each index of `groups`. The reference program is written for one: setup_inputs(seed, part) draws one part's arguments, and reference() takes and returns one part's arrays. A program takes and returns all parts, laid end to end along the dimension named above; an argument that names none is the same for every part. Nothing has to cross between parts.
Inputs may be any that keep to these rules, and one draw needn't show every extreme that they name: `mem_pos`: each membrane point lies within 0.7 of the vessel axis (first two coordinates) with third coordinate between 0 and 8. `wall_pos`: each wall point lies on the unit cylinder around the vessel axis, third coordinate between 0 and 8. `wall_normal`: column w is the outward unit normal of the cylinder at wall_pos[:, w] times 16 pi / 512.
All inputs are finite; a program needn't handle non-finite values.
Results may differ from the reference program's by a relative error of at most 0.002.
Values may be sent and summed in bfloat16 or wider, within the bound.
A program may use at most 64 MiB of HBM per device.

```python
import math
import jax
import jax.numpy as jnp
from jax import lax

COLS = 32
HALF = 16
MEMBRANE = 1024
WALLS = 512


def draw_mem_pos(key, part):
    key_radius, key_angle, key_height = jax.random.split(jax.random.fold_in(key, 11), 3)
    uniform_draw = jax.random.uniform(key_radius, (MEMBRANE,), jnp.float32)
    radius = 0.7 * jnp.sqrt(uniform_draw)
    angle = jax.random.uniform(key_angle, (MEMBRANE,), jnp.float32, -math.pi, math.pi)
    height = jax.random.uniform(key_height, (MEMBRANE,), jnp.float32, 0.0, 8.0)
    return jnp.stack([radius * jnp.cos(angle), radius * jnp.sin(angle), height])


def wall_layout(key):
    key_angle, key_height = jax.random.split(jax.random.fold_in(key, 23))
    angle = jax.random.uniform(key_angle, (WALLS,), jnp.float32, -math.pi, math.pi)
    height = jax.random.uniform(key_height, (WALLS,), jnp.float32, 0.0, 8.0)
    return (angle, height)


def draw_wall_pos(key, part):
    angle, height = wall_layout(key)
    return jnp.stack([jnp.cos(angle), jnp.sin(angle), height])


def draw_wall_normal(key, part):
    angle, height = wall_layout(key)
    area = 16.0 * math.pi / WALLS
    return jnp.stack([jnp.cos(angle), jnp.sin(angle), jnp.zeros_like(height)]) * area


def level_of(key, shape, cuts, low, top_value):
    def one(axis_at, shards_of):
        draws = jax.random.uniform(jax.random.fold_in(jax.random.fold_in(key, 6), axis_at), (shards_of,), jnp.float32, low / len(cuts), top_value / len(cuts))
        return jnp.repeat(jnp.exp(draws), shape[axis_at] // shards_of).reshape((-1,) + (1,) * (len(shape) - axis_at - 1))

    loudness = one(*cuts[0])
    for cut in cuts[1:]:
        loudness = loudness * one(*cut)
    return loudness


def scatter_about(rng, dims, scale, most, shards=(), kind=jnp.bfloat16):
    entries = scale * jax.random.normal(rng, dims, jnp.float32)
    if shards:
        entries = entries * level_of(rng, dims, shards, -0.22, 0.18)
    return jnp.clip(entries, -most, most).astype(kind)


def setup_inputs(seed: int = 0, part: int = 0) -> dict:
    arg_keys = jax.random.split(jax.random.key(seed), 8)
    part_splits = jax.random.split(jax.random.fold_in(arg_keys[7], part), 8)
    mem_pos = draw_mem_pos(jax.random.fold_in(jax.random.fold_in(arg_keys[7], part), 71), part)
    forces = scatter_about(part_splits[1], (COLS, 3, MEMBRANE), 0.2, 1.59375, ((2, 16),))
    wall_pos = draw_wall_pos(jax.random.fold_in(jax.random.fold_in(arg_keys[7], part), 71), part)
    wall_normal = draw_wall_normal(jax.random.fold_in(jax.random.fold_in(arg_keys[7], part), 71), part)
    wall_data = scatter_about(part_splits[4], (COLS, 3, WALLS), 1.0, 6.0, ((2, 4),), jnp.float32)
    lag_density = scatter_about(part_splits[5], (HALF, 3, WALLS), 3.0, 15.0, ((2, 16),))
    batch_order = jax.random.permutation(arg_keys[6], COLS).astype(jnp.int32)
    return dict(mem_pos=mem_pos, forces=forces, wall_pos=wall_pos, wall_normal=wall_normal, wall_data=wall_data, lag_density=lag_density, batch_order=batch_order)


stokes_coef = 1.0 / (8.0 * math.pi)

def single_tile(targets, sources):
    separation = targets[:, None, :] - sources[:, :, None]
    inverse = lax.rsqrt(lax.optimization_barrier(jnp.sum(separation * separation, axis=0)))
    inverse_cube = inverse * inverse * inverse
    stacked = []
    for second_dim in range(3):
        entries_row = []
        for first_dim in range(3):
            element = separation[first_dim] * separation[second_dim] * inverse_cube
            if first_dim == second_dim:
                element = element + inverse
            entries_row.append(element * stokes_coef)
        stacked.append(jnp.stack(entries_row, axis=1))
    kernel_tile = jnp.stack(stacked, axis=0)
    return kernel_tile.reshape(3 * sources.shape[1], 3 * targets.shape[1]).astype(jnp.bfloat16)

def double_tile(targets, sources, normals):
    separation = targets[:, None, :] - sources[:, :, None]
    inverse = lax.rsqrt(lax.optimization_barrier(jnp.sum(separation * separation, axis=0)))
    normal_flux = lax.optimization_barrier(jnp.sum(separation * normals[:, :, None], axis=0))
    weight = -6.0 * stokes_coef * normal_flux * inverse ** 5
    stacked = []
    for second_dim in range(3):
        entries_row = []
        for first_dim in range(3):
            entries_row.append(weight * separation[first_dim] * separation[second_dim])
        stacked.append(jnp.stack(entries_row, axis=1))
    kernel_tile = jnp.stack(stacked, axis=0)
    return kernel_tile.reshape(3 * sources.shape[1], 3 * targets.shape[1]).astype(jnp.bfloat16)

def reference(mem_pos, forces, wall_pos, wall_normal, wall_data, lag_density, batch_order):
    columns = forces.shape[0]
    halfway = columns // 2
    point_count = mem_pos.shape[1]
    wall_count = wall_pos.shape[1]
    piece_len = math.gcd(point_count, 128)
    block_count = point_count // piece_len

    def add_single(running, block_index):
        offset = (block_index * piece_len).astype(jnp.int32)
        position = lax.dynamic_slice_in_dim(mem_pos, offset, piece_len, 1)
        loaded = lax.dynamic_slice_in_dim(forces, offset, piece_len, 2).reshape(columns, 3 * piece_len)
        return (running + jnp.dot(loaded, single_tile(wall_pos, position), preferred_element_type=jnp.float32), None)
    running, _ = lax.scan(add_single, jnp.zeros((columns, 3 * wall_count), jnp.float32), jnp.arange(block_count, dtype=jnp.int32))
    wall_velocity = running.reshape(columns, 3, wall_count)
    density = 2.0 * (wall_data - wall_velocity)
    first = jnp.take(density, batch_order[:halfway], axis=0).astype(jnp.bfloat16)
    wall_density = jnp.take(density, batch_order[halfway:], axis=0)
    carried = jnp.concatenate([lag_density, first], axis=0).reshape(columns, 3 * wall_count)

    def one_block(block_index):
        offset = (block_index * piece_len).astype(jnp.int32)
        position = lax.dynamic_slice_in_dim(mem_pos, offset, piece_len, 1)
        product = jnp.dot(carried, double_tile(position, wall_pos, wall_normal), preferred_element_type=jnp.float32)
        return product.reshape(columns, 3, piece_len)
    pieces = lax.map(one_block, jnp.arange(block_count, dtype=jnp.int32))
    batched = jnp.transpose(pieces, (1, 2, 0, 3)).reshape(columns, 3, point_count)
    membrane_velocity = jnp.zeros_like(batched).at[batch_order].set(batched)
    return (membrane_velocity, wall_density)
```

```python
import functools
import math

import jax
import jax.numpy as jnp
from jax import lax
from jax.experimental import pallas as pl
from jax.experimental.pallas import tpu as pltpu
from jax.sharding import PartitionSpec as P

stokes_coef = 1.0 / (8.0 * math.pi)


def single_tile(targets, sources):
    separation = targets[:, None, :] - sources[:, :, None]
    inverse = lax.rsqrt(jnp.sum(separation * separation, axis=0))
    inverse_cube = inverse * inverse * inverse
    stacked = []
    for second_dim in range(3):
        entries_row = []
        for first_dim in range(3):
            element = separation[first_dim] * separation[second_dim] * inverse_cube
            if first_dim == second_dim:
                element = element + inverse
            entries_row.append(element * stokes_coef)
        stacked.append(jnp.stack(entries_row, axis=1))
    kernel_tile = jnp.stack(stacked, axis=0)
    return kernel_tile.reshape(3 * sources.shape[1], 3 * targets.shape[1]).astype(jnp.bfloat16)


def double_tile(targets, sources, normals):
    separation = targets[:, None, :] - sources[:, :, None]
    inverse = lax.rsqrt(jnp.sum(separation * separation, axis=0))
    normal_flux = jnp.sum(separation * normals[:, :, None], axis=0)
    weight = -6.0 * stokes_coef * normal_flux * inverse**5
    stacked = []
    for second_dim in range(3):
        entries_row = []
        for first_dim in range(3):
            entries_row.append(weight * separation[first_dim] * separation[second_dim])
        stacked.append(jnp.stack(entries_row, axis=1))
    kernel_tile = jnp.stack(stacked, axis=0)
    return kernel_tile.reshape(3 * sources.shape[1], 3 * targets.shape[1]).astype(jnp.bfloat16)


def shards(mem_pos, forces, wall_pos, wall_normal, wall_data, lag_density, batch_order):
    columns = forces.shape[0]
    halfway = columns // 2
    point_count = mem_pos.shape[1]
    wall_count = wall_pos.shape[1]
    shard_width = lag_density.shape[2]
    piece_len = math.gcd(point_count, 128)
    block_count = point_count // piece_len
    first_rows = batch_order[:halfway]
    second_rows = batch_order[halfway:]
    force_block = lax.all_gather(forces, "wall", axis=2, tiled=True)
    lag_block = lax.all_gather(lag_density, "cell", axis=2, tiled=True)
    lag_flat = lag_block.reshape(halfway, 3 * wall_count)

    def position_at(block_index):
        return lax.dynamic_slice_in_dim(mem_pos, block_index * piece_len, piece_len, 1)

    def single_term(block_index):
        loaded = lax.dynamic_slice_in_dim(force_block, block_index * piece_len, piece_len, 2)
        loaded = loaded.reshape(columns, 3 * piece_len)
        return jnp.dot(
            loaded,
            single_tile(wall_pos, position_at(block_index)),
            preferred_element_type=jnp.float32,
        )

    def double_term(dense_rows, block_index):
        kernel_tile = double_tile(position_at(block_index), wall_pos, wall_normal)
        product = jnp.dot(dense_rows, kernel_tile, preferred_element_type=jnp.float32)
        return product.reshape(dense_rows.shape[0], 3, piece_len)

    def place_block(target, piece, block_index):
        return lax.dynamic_update_slice_in_dim(target, piece, block_index * piece_len, 2)

    empty_wall = jnp.zeros((columns, 3 * wall_count), jnp.float32)

    def add_single(block_index, running):
        return running + single_term(block_index)

    running = lax.fori_loop(0, block_count, add_single, empty_wall)
    wall_term = running.reshape(columns, 3, wall_count)
    position_cell = lax.axis_index("cell")
    first_sum = lax.psum(jnp.take(wall_term, first_rows, axis=0), "cell")
    first_block = (2.0 * (jnp.take(wall_data, first_rows, axis=0) - first_sum)).astype(jnp.bfloat16)
    second_sum = lax.psum_scatter(
        jnp.take(wall_term, second_rows, axis=0).astype(jnp.bfloat16),
        "cell",
        scatter_dimension=2,
        tiled=True,
    ).astype(jnp.float32)
    second_data = lax.dynamic_slice_in_dim(
        jnp.take(wall_data, second_rows, axis=0), position_cell * shard_width, shard_width, 2
    )
    wall_density = 2.0 * (second_data - second_sum)
    first_flat = first_block.reshape(halfway, 3 * wall_count)
    carried = jnp.concatenate([lag_flat, first_flat], axis=0)

    def all_terms(block_index, target):
        return place_block(target, double_term(carried, block_index), block_index)

    membrane_term = lax.fori_loop(
        0, block_count, all_terms, jnp.zeros((columns, 3, point_count), jnp.float32)
    )
    batched = lax.psum_scatter(membrane_term, "wall", scatter_dimension=2, tiled=True)
    membrane_velocity = jnp.zeros_like(batched).at[batch_order].set(batched)
    return (membrane_velocity, wall_density)

LANES = 128
MESH = pl.DeviceIdType.MESH
NT = (((1,), (1,)), ((), ()))


def nearest(position, rank, count):
    mirrored = position >= (count + 1) // 2
    here = jnp.where(mirrored, count - 1 - position, position)
    other = jnp.where(rank <= here, rank - 1, rank)
    return jnp.where(mirrored, count - 1 - other, other)


def fused_kernel(
    cells,
    walls,
    mem_ref,
    force_ref,
    wall_ref,
    normal_ref,
    data_ref,
    lag_ref,
    order_ref,
    out_ref,
    density_ref,
    blocks,
    mem_all,
    wall_all,
    normal_all,
    first_all,
    wall_cols,
    mem_cols,
    single_all,
    double_all,
    block_send,
    block_recv,
    forward_send,
    mem_send,
    mem_recv,
    pos_send,
    pos_recv,
    first_send,
    first_recv,
):
    cell = lax.axis_index("cell")
    wall = lax.axis_index("wall")
    columns = order_ref.shape[1]
    halfway = columns // 2
    point_count = mem_ref.shape[1]
    wall_count = wall_ref.shape[1]
    own_points = force_ref.shape[2]
    shard_width = lag_ref.shape[2]

    cell_peers = [lax.rem(cell + step, cells) for step in range(1, cells)]
    wall_peers = [lax.rem(wall + step, walls) for step in range(1, walls)]

    barrier = pltpu.get_barrier_semaphore()
    for peer in cell_peers:
        pl.semaphore_signal(barrier, inc=1, device_id={"cell": peer}, device_id_type=MESH)
    for peer in wall_peers:
        pl.semaphore_signal(barrier, inc=1, device_id={"wall": peer}, device_id_type=MESH)

    order_row = order_ref[...]
    row_ids = lax.broadcasted_iota(jnp.int32, (columns, columns), 0)
    col_ids = lax.broadcasted_iota(jnp.int32, (columns, columns), 1)
    scatter = (row_ids == order_row).astype(jnp.float32).astype(jnp.bfloat16)
    unit = (row_ids == col_ids).astype(jnp.float32).astype(jnp.bfloat16)
    gather_f32 = lax.dot_general(unit, scatter, NT, preferred_element_type=jnp.float32)
    gather = gather_f32.astype(jnp.bfloat16)

    for j in range(3):
        rows = jnp.dot(gather, force_ref[j], preferred_element_type=jnp.float32)
        packed = jnp.concatenate([rows[:halfway], rows[halfway:]], axis=1)
        blocks[cell, wall, j] = packed.astype(jnp.bfloat16)
    lag_rows = [lag_ref[j].astype(jnp.float32) for j in range(3)]
    room = 2 * own_points - 3 * shard_width
    lag_rows.append(jnp.zeros((halfway, room), jnp.float32))
    blocks[cell, wall, 3] = jnp.concatenate(lag_rows, axis=1).astype(jnp.bfloat16)
    mem_all[cell] = mem_ref[...]
    wall_all[wall] = wall_ref[...]
    normal_all[wall] = normal_ref[...]

    def block_copy(source, to_cell, rank):
        return pltpu.make_async_remote_copy(
            blocks.at[source, wall],
            blocks.at[source, wall],
            block_send.at[rank],
            block_recv.at[source, wall],
            device_id={"cell": to_cell},
            device_id_type=MESH,
        )

    def forward_copy(source_cell, source_wall, to_wall, rank, slot):
        return pltpu.make_async_remote_copy(
            blocks.at[source_cell, source_wall],
            blocks.at[source_cell, source_wall],
            forward_send.at[rank, slot],
            block_recv.at[source_cell, source_wall],
            device_id={"wall": to_wall},
            device_id_type=MESH,
        )

    def mem_copy(source, to_cell, rank):
        return pltpu.make_async_remote_copy(
            mem_ref,
            mem_all.at[source],
            mem_send.at[rank],
            mem_recv.at[source],
            device_id={"cell": to_cell},
            device_id_type=MESH,
        )

    def pos_copies(source, to_wall, rank):
        return [
            pltpu.make_async_remote_copy(
                given,
                held.at[source],
                pos_send.at[rank, kind],
                pos_recv.at[source, kind],
                device_id={"wall": to_wall},
                device_id_type=MESH,
            )
            for kind, (given, held) in enumerate(((wall_ref, wall_all), (normal_ref, normal_all)))
        ]

    def first_copy(source, to_wall, rank):
        return pltpu.make_async_remote_copy(
            first_all.at[source],
            first_all.at[source],
            first_send.at[rank],
            first_recv.at[source],
            device_id={"wall": to_wall},
            device_id_type=MESH,
        )

    pl.semaphore_wait(barrier, cells + walls - 2)

    sent = []
    for rank in range(cells - 1):
        sent.append(block_copy(cell, nearest(cell, cells - 1 - rank, cells), rank))
        sent[-1].start()
    for rank, peer in enumerate(wall_peers):
        sent.append(forward_copy(cell, wall, peer, 0, rank))
        sent[-1].start()
    for rank, peer in enumerate(cell_peers):
        sent.append(mem_copy(cell, peer, rank))
        sent[-1].start()
    for rank, peer in enumerate(wall_peers):
        for copy in pos_copies(wall, peer, rank):
            sent.append(copy)
            copy.start()

    data_rows = [
        jnp.dot(gather_f32, data_ref[j], precision=lax.Precision.HIGHEST) for j in range(3)
    ]
    for j in range(3):
        wall_cols[j] = jnp.broadcast_to(wall_ref[j : j + 1, :], (LANES, wall_count)).T
        mem_cols[j] = jnp.broadcast_to(mem_ref[j : j + 1, :], (LANES, point_count)).T

    def fill_single(source):
        for start in range(0, point_count, LANES):
            apart = [
                wall_cols[j] - mem_all[source, j : j + 1, start : start + LANES] for j in range(3)
            ]
            square = apart[0] * apart[0] + apart[1] * apart[1] + apart[2] * apart[2]
            inverse = lax.rsqrt(square)
            scaled = stokes_coef * inverse
            cube = scaled * (inverse * inverse)
            for j in range(3):
                along = apart[j] * cube
                for i in range(j + 1):
                    element = along * apart[i]
                    if i == j:
                        element = element + scaled
                    element = element.astype(jnp.bfloat16)
                    for a, b in {(i, j), (j, i)}:
                        single_all[
                            source,
                            a * wall_count : (a + 1) * wall_count,
                            b * point_count + start : b * point_count + start + LANES,
                        ] = element

    def fill_double(source):
        own = pl.ds(pl.multiple_of(wall * own_points, own_points), own_points)
        for start in range(0, wall_count, LANES):
            apart = [
                mem_cols[j, own, :] - wall_all[source, j : j + 1, start : start + LANES]
                for j in range(3)
            ]
            square = apart[0] * apart[0] + apart[1] * apart[1] + apart[2] * apart[2]
            inverse = lax.rsqrt(square)
            flux = (
                apart[0] * normal_all[source, 0:1, start : start + LANES]
                + apart[1] * normal_all[source, 1:2, start : start + LANES]
                + apart[2] * normal_all[source, 2:3, start : start + LANES]
            )
            inverse_square = inverse * inverse
            fifth = inverse_square * inverse_square * inverse
            weight = (-6.0 * stokes_coef) * flux * fifth
            for j in range(3):
                along = apart[j] * weight
                for i in range(j + 1):
                    element = (along * apart[i]).astype(jnp.bfloat16)
                    for a, b in {(i, j), (j, i)}:
                        double_all[
                            source,
                            a * own_points : (a + 1) * own_points,
                            b * wall_count + start : b * wall_count + start + LANES,
                        ] = element

    fill_single(cell)
    fill_double(wall)

    for rank in range(1, cells):
        source = nearest(cell, rank, cells)
        block_copy(source, source, 0).wait_recv()
        for slot, peer in enumerate(wall_peers):
            sent.append(forward_copy(source, wall, peer, rank, slot))
            sent[-1].start()
        mem_copy(source, source, 0).wait_recv()
        fill_single(source)
        if rank == 1:
            for peer in wall_peers:
                for copy in pos_copies(peer, peer, 0):
                    copy.wait_recv()
                fill_double(peer)

    velocity = jnp.zeros((columns, 3 * wall_count), jnp.float32)
    for rank in range(cells):
        source = cell if rank == 0 else nearest(cell, rank, cells)
        for peer in wall_peers:
            forward_copy(source, peer, peer, 0, 0).wait_recv()
        loaded = []
        for j in range(3):
            pieces = [blocks[source, k, j] for k in range(walls)]
            upper = jnp.concatenate([piece[:, :own_points] for piece in pieces], axis=1)
            lower = jnp.concatenate([piece[:, own_points:] for piece in pieces], axis=1)
            loaded.append(jnp.concatenate([upper, lower], axis=0))
        velocity = velocity + lax.dot_general(
            jnp.concatenate(loaded, axis=1),
            single_all[source],
            NT,
            preferred_element_type=jnp.float32,
        )

    density = [
        2.0 * (data_rows[j] - velocity[:, j * wall_count : (j + 1) * wall_count])
        for j in range(3)
    ]
    for j in range(3):
        first_all[wall, j] = density[j][:halfway].astype(jnp.bfloat16)
    for rank, peer in enumerate(wall_peers):
        sent.append(first_copy(wall, peer, rank))
        sent[-1].start()

    shift = lax.rem((cells - cell) * shard_width, wall_count)
    for j in range(3):
        density_ref[j] = pltpu.roll(density[j][halfway:], shift, 1)[:, :shard_width]

    total = jnp.zeros((columns, 3 * own_points), jnp.float32)
    for source in range(walls):
        lag = jnp.concatenate(
            [
                blocks[k, source, 3, :, j * shard_width : (j + 1) * shard_width]
                for j in range(3)
                for k in range(cells)
            ],
            axis=1,
        )
        placed = jnp.dot(scatter[:, :halfway], lag, preferred_element_type=jnp.float32)
        total = total + lax.dot_general(
            placed.astype(jnp.bfloat16), double_all[source], NT, preferred_element_type=jnp.float32
        )

    for rank in range(walls):
        source = wall
        if rank:
            source = wall_peers[rank - 1]
            first_copy(source, source, 0).wait_recv()
        first = jnp.concatenate([first_all[source, j] for j in range(3)], axis=1)
        placed = jnp.dot(scatter[:, halfway:], first, preferred_element_type=jnp.float32)
        total = total + lax.dot_general(
            placed.astype(jnp.bfloat16), double_all[source], NT, preferred_element_type=jnp.float32
        )
    for i in range(3):
        out_ref[i] = total[:, i * own_points : (i + 1) * own_points]

    for copy in sent:
        copy.wait_send()


def fused_shards(cells, walls, mem_pos, forces, wall_pos, wall_normal, wall_data, lag_density, batch_order):
    columns = forces.shape[0]
    halfway = columns // 2
    point_count = mem_pos.shape[1]
    wall_count = wall_pos.shape[1]
    own_points = forces.shape[2]
    shard_width = lag_density.shape[2]
    dma = pltpu.SemaphoreType.DMA
    vmem = pl.BlockSpec(memory_space=pltpu.VMEM)
    velocity, density = pl.pallas_call(
        functools.partial(fused_kernel, cells, walls),
        out_shape=(
            jax.ShapeDtypeStruct((3, columns, own_points), jnp.float32),
            jax.ShapeDtypeStruct((3, halfway, shard_width), jnp.float32),
        ),
        in_specs=[vmem] * 7,
        out_specs=(vmem, vmem),
        scratch_shapes=[
            pltpu.VMEM((cells, walls, 4, halfway, 2 * own_points), jnp.bfloat16),
            pltpu.VMEM((cells, 3, point_count), jnp.float32),
            pltpu.VMEM((walls, 3, wall_count), jnp.float32),
            pltpu.VMEM((walls, 3, wall_count), jnp.float32),
            pltpu.VMEM((walls, 3, halfway, wall_count), jnp.bfloat16),
            pltpu.VMEM((3, wall_count, LANES), jnp.float32),
            pltpu.VMEM((3, point_count, LANES), jnp.float32),
            pltpu.VMEM((cells, 3 * wall_count, 3 * point_count), jnp.bfloat16),
            pltpu.VMEM((walls, 3 * own_points, 3 * wall_count), jnp.bfloat16),
            dma((cells,)),
            dma((cells, walls)),
            dma((cells, walls)),
            dma((cells,)),
            dma((cells,)),
            dma((walls, 2)),
            dma((walls, 2)),
            dma((walls,)),
            dma((walls,)),
        ],
        compiler_params=pltpu.CompilerParams(
            collective_id=0, has_side_effects=True, vmem_limit_bytes=VMEM_GRANT
        ),
        name="coupling",
    )(
        mem_pos,
        jnp.transpose(forces, (1, 0, 2)),
        wall_pos,
        wall_normal,
        jnp.transpose(wall_data, (1, 0, 2)),
        jnp.transpose(lag_density, (1, 0, 2)),
        batch_order.reshape(1, columns),
    )
    return (jnp.transpose(velocity, (1, 0, 2)), jnp.transpose(density, (1, 0, 2)))


VMEM_GRANT = 32 * 1024 * 1024


def step(cells, walls, mem_pos, forces, wall_pos, *rest):
    point_count = mem_pos.shape[1]
    wall_count = wall_pos.shape[1]
    own_points = forces.shape[2]
    shard_width = rest[2].shape[2]
    tiles = 18 * wall_count * (cells * point_count + walls * own_points)
    fits = tiles <= VMEM_GRANT // 2
    aligned = (
        point_count % LANES == 0
        and wall_count % LANES == 0
        and 2 * own_points == LANES
        and 3 * shard_width <= LANES
    )
    if fits and aligned:
        return fused_shards(cells, walls, mem_pos, forces, wall_pos, *rest)
    return shards(mem_pos, forces, wall_pos, *rest)


def solution(mesh):
    placed = (
        P(None, ("groups", "cell")),
        P(None, None, ("groups", "cell", "wall")),
        P(None, ("groups", "wall")),
        P(None, ("groups", "wall")),
        P(None, None, ("groups", "wall")),
        P(None, None, ("groups", "wall", "cell")),
        P(),
    )
    return jax.shard_map(
        functools.partial(step, mesh.shape["cell"], mesh.shape["wall"]),
        mesh=mesh,
        in_specs=placed,
        out_specs=(
            P(None, None, ("groups", "cell", "wall")),
            P(None, None, ("groups", "wall", "cell")),
        ),
        check_vma=False,
    )
```

```python
import functools
import math

import jax
import jax.numpy as jnp
from jax import lax
from jax.experimental import pallas as pl
from jax.experimental.pallas import tpu as pltpu
from jax.sharding import PartitionSpec as P

stokes_coef = 1.0 / (8.0 * math.pi)


def single_tile(targets, sources):
    separation = targets[:, None, :] - sources[:, :, None]
    inverse = lax.rsqrt(jnp.sum(separation * separation, axis=0))
    inverse_cube = inverse * inverse * inverse
    stacked = []
    for second_dim in range(3):
        entries_row = []
        for first_dim in range(3):
            element = separation[first_dim] * separation[second_dim] * inverse_cube
            if first_dim == second_dim:
                element = element + inverse
            entries_row.append(element * stokes_coef)
        stacked.append(jnp.stack(entries_row, axis=1))
    kernel_tile = jnp.stack(stacked, axis=0)
    return kernel_tile.reshape(3 * sources.shape[1], 3 * targets.shape[1]).astype(jnp.bfloat16)


def double_tile(targets, sources, normals):
    separation = targets[:, None, :] - sources[:, :, None]
    inverse = lax.rsqrt(jnp.sum(separation * separation, axis=0))
    normal_flux = jnp.sum(separation * normals[:, :, None], axis=0)
    weight = -6.0 * stokes_coef * normal_flux * inverse**5
    stacked = []
    for second_dim in range(3):
        entries_row = []
        for first_dim in range(3):
            entries_row.append(weight * separation[first_dim] * separation[second_dim])
        stacked.append(jnp.stack(entries_row, axis=1))
    kernel_tile = jnp.stack(stacked, axis=0)
    return kernel_tile.reshape(3 * sources.shape[1], 3 * targets.shape[1]).astype(jnp.bfloat16)


def shards(mem_pos, forces, wall_pos, wall_normal, wall_data, lag_density, batch_order):
    columns = forces.shape[0]
    halfway = columns // 2
    point_count = mem_pos.shape[1]
    wall_count = wall_pos.shape[1]
    shard_width = lag_density.shape[2]
    piece_len = math.gcd(point_count, 128)
    block_count = point_count // piece_len
    first_rows = batch_order[:halfway]
    second_rows = batch_order[halfway:]
    force_block = lax.all_gather(forces, "wall", axis=2, tiled=True)
    lag_block = lax.all_gather(lag_density, "cell", axis=2, tiled=True)
    lag_flat = lag_block.reshape(halfway, 3 * wall_count)

    def position_at(block_index):
        return lax.dynamic_slice_in_dim(mem_pos, block_index * piece_len, piece_len, 1)

    def single_term(block_index):
        loaded = lax.dynamic_slice_in_dim(force_block, block_index * piece_len, piece_len, 2)
        loaded = loaded.reshape(columns, 3 * piece_len)
        return jnp.dot(
            loaded,
            single_tile(wall_pos, position_at(block_index)),
            preferred_element_type=jnp.float32,
        )

    def double_term(dense_rows, block_index):
        kernel_tile = double_tile(position_at(block_index), wall_pos, wall_normal)
        product = jnp.dot(dense_rows, kernel_tile, preferred_element_type=jnp.float32)
        return product.reshape(dense_rows.shape[0], 3, piece_len)

    def place_block(target, piece, block_index):
        return lax.dynamic_update_slice_in_dim(target, piece, block_index * piece_len, 2)

    empty_wall = jnp.zeros((columns, 3 * wall_count), jnp.float32)

    def add_single(block_index, running):
        return running + single_term(block_index)

    running = lax.fori_loop(0, block_count, add_single, empty_wall)
    wall_term = running.reshape(columns, 3, wall_count)
    position_cell = lax.axis_index("cell")
    first_sum = lax.psum(jnp.take(wall_term, first_rows, axis=0), "cell")
    first_block = (2.0 * (jnp.take(wall_data, first_rows, axis=0) - first_sum)).astype(jnp.bfloat16)
    second_sum = lax.psum_scatter(
        jnp.take(wall_term, second_rows, axis=0).astype(jnp.bfloat16),
        "cell",
        scatter_dimension=2,
        tiled=True,
    ).astype(jnp.float32)
    second_data = lax.dynamic_slice_in_dim(
        jnp.take(wall_data, second_rows, axis=0), position_cell * shard_width, shard_width, 2
    )
    wall_density = 2.0 * (second_data - second_sum)
    first_flat = first_block.reshape(halfway, 3 * wall_count)
    carried = jnp.concatenate([lag_flat, first_flat], axis=0)

    def all_terms(block_index, target):
        return place_block(target, double_term(carried, block_index), block_index)

    membrane_term = lax.fori_loop(
        0, block_count, all_terms, jnp.zeros((columns, 3, point_count), jnp.float32)
    )
    batched = lax.psum_scatter(membrane_term, "wall", scatter_dimension=2, tiled=True)
    membrane_velocity = jnp.zeros_like(batched).at[batch_order].set(batched)
    return (membrane_velocity, wall_density)

LANES = 128
MESH = pl.DeviceIdType.MESH
NT = (((1,), (1,)), ((), ()))


def nearest(position, rank, count):
    mirrored = position >= (count + 1) // 2
    here = jnp.where(mirrored, count - 1 - position, position)
    other = jnp.where(rank <= here, rank - 1, rank)
    return jnp.where(mirrored, count - 1 - other, other)


def fused_kernel(
    cells,
    walls,
    mem_hbm,
    force_hbm,
    wall_hbm,
    normal_hbm,
    data_hbm,
    lag_hbm,
    order_hbm,
    out_ref,
    density_ref,
    force_ref,
    data_ref,
    lag_ref,
    order_ref,
    blocks,
    mem_all,
    wall_all,
    normal_all,
    first_all,
    wall_cols,
    mem_cols,
    single_all,
    double_all,
    load_sem,
    block_send,
    block_recv,
    forward_send,
    mem_send,
    mem_recv,
    pos_send,
    pos_recv,
    first_send,
    first_recv,
):
    cell = lax.axis_index("cell")
    wall = lax.axis_index("wall")
    columns = order_ref.shape[1]
    halfway = columns // 2
    point_count = mem_hbm.shape[1]
    wall_count = wall_hbm.shape[1]
    own_points = force_ref.shape[2]
    shard_width = lag_ref.shape[2]

    loads = [
        pltpu.make_async_copy(given, held, load_sem.at[at])
        for at, (given, held) in enumerate(
            (
                (order_hbm, order_ref),
                (force_hbm, force_ref),
                (lag_hbm, lag_ref),
                (mem_hbm, mem_all.at[cell]),
                (wall_hbm, wall_all.at[wall]),
                (normal_hbm, normal_all.at[wall]),
                (data_hbm, data_ref),
            )
        )
    ]
    for load in loads:
        load.start()

    cell_peers = [lax.rem(cell + step, cells) for step in range(1, cells)]
    wall_peers = [lax.rem(wall + step, walls) for step in range(1, walls)]

    barrier = pltpu.get_barrier_semaphore()
    for peer in cell_peers:
        pl.semaphore_signal(barrier, inc=1, device_id={"cell": peer}, device_id_type=MESH)
    for peer in wall_peers:
        pl.semaphore_signal(barrier, inc=1, device_id={"wall": peer}, device_id_type=MESH)

    loads[0].wait()
    order_row = order_ref[...]
    row_ids = lax.broadcasted_iota(jnp.int32, (columns, columns), 0)
    col_ids = lax.broadcasted_iota(jnp.int32, (columns, columns), 1)
    scatter = (row_ids == order_row).astype(jnp.float32).astype(jnp.bfloat16)
    unit = (row_ids == col_ids).astype(jnp.float32).astype(jnp.bfloat16)
    gather_f32 = lax.dot_general(unit, scatter, NT, preferred_element_type=jnp.float32)
    gather = gather_f32.astype(jnp.bfloat16)

    loads[1].wait()
    rows = [jnp.dot(gather, force_ref[j], preferred_element_type=jnp.float32) for j in range(3)]
    loads[2].wait()
    lag_rows = [lag_ref[j].astype(jnp.float32) for j in range(3)]
    spare = jnp.zeros((halfway, own_points - 2 * shard_width), jnp.float32)
    unused = jnp.zeros((halfway, own_points - shard_width), jnp.float32)
    halves = (
        ([row[:halfway] for row in rows], (lag_rows[0], lag_rows[1], spare)),
        ([row[halfway:] for row in rows], (lag_rows[2], unused)),
    )
    for wave, (part, rest) in enumerate(halves):
        rest = [piece for piece in rest if piece.shape[1]]
        pair = jnp.concatenate([part[0], part[1]], axis=1)
        blocks[wave, cell, wall, 0] = pair.astype(jnp.bfloat16)
        pair = jnp.concatenate([part[2], *rest], axis=1)
        blocks[wave, cell, wall, 1] = pair.astype(jnp.bfloat16)
    for load in loads[3:6]:
        load.wait()

    def block_copy(wave, source, to_cell, rank):
        return pltpu.make_async_remote_copy(
            blocks.at[wave, source, wall],
            blocks.at[wave, source, wall],
            block_send.at[wave, rank],
            block_recv.at[wave, source, wall],
            device_id={"cell": to_cell},
            device_id_type=MESH,
        )

    def forward_copy(wave, source_cell, source_wall, to_wall, rank, slot):
        return pltpu.make_async_remote_copy(
            blocks.at[wave, source_cell, source_wall],
            blocks.at[wave, source_cell, source_wall],
            forward_send.at[wave, rank, slot],
            block_recv.at[wave, source_cell, source_wall],
            device_id={"wall": to_wall},
            device_id_type=MESH,
        )

    def mem_copy(source, to_cell, rank):
        return pltpu.make_async_remote_copy(
            mem_all.at[source],
            mem_all.at[source],
            mem_send.at[rank],
            mem_recv.at[source],
            device_id={"cell": to_cell},
            device_id_type=MESH,
        )

    def pos_copies(source, to_wall, rank):
        return [
            pltpu.make_async_remote_copy(
                held.at[source],
                held.at[source],
                pos_send.at[rank, kind],
                pos_recv.at[source, kind],
                device_id={"wall": to_wall},
                device_id_type=MESH,
            )
            for kind, held in enumerate((wall_all, normal_all))
        ]

    def first_copy(source, to_wall, rank):
        return pltpu.make_async_remote_copy(
            first_all.at[source],
            first_all.at[source],
            first_send.at[rank],
            first_recv.at[source],
            device_id={"wall": to_wall},
            device_id_type=MESH,
        )

    pl.semaphore_wait(barrier, cells + walls - 2)

    sent = []

    def send(copy):
        sent.append(copy)
        copy.start()

    def send_own(wave):
        for rank in range(cells - 1):
            send(block_copy(wave, cell, nearest(cell, cells - 1 - rank, cells), rank))
        for slot, peer in enumerate(wall_peers):
            send(forward_copy(wave, cell, wall, peer, 0, slot))

    def pass_on(wave, rank):
        source = nearest(cell, rank, cells)
        block_copy(wave, source, source, 0).wait_recv()
        for slot, peer in enumerate(wall_peers):
            send(forward_copy(wave, source, wall, peer, rank, slot))

    send_own(0)
    for rank, peer in enumerate(cell_peers):
        send(mem_copy(cell, peer, rank))
    for rank, peer in enumerate(wall_peers):
        for copy in pos_copies(wall, peer, rank):
            send(copy)
    send_own(1)

    for j in range(3):
        wall_cols[j] = jnp.broadcast_to(wall_all[wall, j : j + 1, :], (LANES, wall_count)).T
        mem_cols[j] = jnp.broadcast_to(mem_all[cell, j : j + 1, :], (LANES, point_count)).T
    loads[6].wait()

    def fill_single(source):
        for start in range(0, point_count, LANES):
            apart = [
                wall_cols[j] - mem_all[source, j : j + 1, start : start + LANES] for j in range(3)
            ]
            square = apart[0] * apart[0] + apart[1] * apart[1] + apart[2] * apart[2]
            inverse = lax.rsqrt(square)
            scaled = stokes_coef * inverse
            cube = scaled * (inverse * inverse)
            for j in range(3):
                along = apart[j] * cube
                for i in range(j + 1):
                    element = along * apart[i]
                    if i == j:
                        element = element + scaled
                    element = element.astype(jnp.bfloat16)
                    for a, b in {(i, j), (j, i)}:
                        single_all[
                            source,
                            a * wall_count : (a + 1) * wall_count,
                            b * point_count + start : b * point_count + start + LANES,
                        ] = element

    def fill_double(source):
        own = pl.ds(pl.multiple_of(wall * own_points, own_points), own_points)
        for start in range(0, wall_count, LANES):
            apart = [
                mem_cols[j, own, :] - wall_all[source, j : j + 1, start : start + LANES]
                for j in range(3)
            ]
            square = apart[0] * apart[0] + apart[1] * apart[1] + apart[2] * apart[2]
            inverse = lax.rsqrt(square)
            flux = (
                apart[0] * normal_all[source, 0:1, start : start + LANES]
                + apart[1] * normal_all[source, 1:2, start : start + LANES]
                + apart[2] * normal_all[source, 2:3, start : start + LANES]
            )
            inverse_square = inverse * inverse
            fifth = inverse_square * inverse_square * inverse
            weight = (-6.0 * stokes_coef) * flux * fifth
            for j in range(3):
                along = apart[j] * weight
                for i in range(j + 1):
                    element = (along * apart[i]).astype(jnp.bfloat16)
                    for a, b in {(i, j), (j, i)}:
                        double_all[
                            source,
                            a * own_points : (a + 1) * own_points,
                            b * wall_count + start : b * wall_count + start + LANES,
                        ] = element

    fill_single(cell)
    fill_double(wall)

    for rank in range(1, cells):
        pass_on(0, rank)
    for rank in range(1, cells):
        source = nearest(cell, rank, cells)
        mem_copy(source, source, 0).wait_recv()
        fill_single(source)
    for rank in range(1, cells):
        pass_on(1, rank)

    def single_layer(wave):
        velocity = jnp.zeros((halfway, 3 * wall_count), jnp.float32)
        for rank in range(cells):
            source = cell if rank == 0 else nearest(cell, rank, cells)
            for peer in wall_peers:
                forward_copy(wave, source, peer, peer, 0, 0).wait_recv()
            pairs = [blocks[wave, source, k, 0] for k in range(walls)]
            thirds = [blocks[wave, source, k, 1] for k in range(walls)]
            loaded = [piece[:, :own_points] for piece in pairs]
            loaded += [piece[:, own_points:] for piece in pairs]
            loaded += [piece[:, :own_points] for piece in thirds]
            velocity = velocity + lax.dot_general(
                jnp.concatenate(loaded, axis=1),
                single_all[source],
                NT,
                preferred_element_type=jnp.float32,
            )
        held = slice(wave * halfway, (wave + 1) * halfway)
        return [
            2.0 * (data_rows[j][held] - velocity[:, j * wall_count : (j + 1) * wall_count])
            for j in range(3)
        ]

    data_rows = [
        jnp.dot(gather_f32, data_ref[j], precision=lax.Precision.HIGHEST) for j in range(3)
    ]
    first_rows = single_layer(0)
    for j in range(3):
        first_all[wall, j] = first_rows[j].astype(jnp.bfloat16)
    for rank, peer in enumerate(wall_peers):
        send(first_copy(wall, peer, rank))

    for peer in wall_peers:
        for copy in pos_copies(peer, peer, 0):
            copy.wait_recv()
        fill_double(peer)
    shift = lax.rem((cells - cell) * shard_width, wall_count)
    second_rows = single_layer(1)
    for j in range(3):
        density_ref[j] = pltpu.roll(second_rows[j], shift, 1)[:, :shard_width]

    lag_places = ((0, own_points), (0, own_points + shard_width), (1, own_points))
    total = jnp.zeros((columns, 3 * own_points), jnp.float32)
    for source in range(walls):
        lag = jnp.concatenate(
            [
                blocks[wave, k, source, 1, :, start : start + shard_width]
                for wave, start in lag_places
                for k in range(cells)
            ],
            axis=1,
        )
        placed = jnp.dot(scatter[:, :halfway], lag, preferred_element_type=jnp.float32)
        total = total + lax.dot_general(
            placed.astype(jnp.bfloat16), double_all[source], NT, preferred_element_type=jnp.float32
        )

    for rank in range(walls):
        source = wall
        if rank:
            source = wall_peers[rank - 1]
            first_copy(source, source, 0).wait_recv()
        first = jnp.concatenate([first_all[source, j] for j in range(3)], axis=1)
        placed = jnp.dot(scatter[:, halfway:], first, preferred_element_type=jnp.float32)
        total = total + lax.dot_general(
            placed.astype(jnp.bfloat16), double_all[source], NT, preferred_element_type=jnp.float32
        )
    for i in range(3):
        out_ref[i] = total[:, i * own_points : (i + 1) * own_points]

    for copy in sent:
        copy.wait_send()


def write_kernel(velocity_ref, density_ref, velocity_hbm, density_hbm, sem):
    first = pltpu.make_async_copy(velocity_ref, velocity_hbm, sem.at[0])
    second = pltpu.make_async_copy(density_ref, density_hbm, sem.at[1])
    first.start()
    second.start()
    first.wait()
    second.wait()


def fused_shards(cells, walls, mem_pos, forces, wall_pos, wall_normal, wall_data, lag_density, batch_order):
    columns = forces.shape[0]
    halfway = columns // 2
    point_count = mem_pos.shape[1]
    wall_count = wall_pos.shape[1]
    own_points = forces.shape[2]
    shard_width = lag_density.shape[2]
    dma = pltpu.SemaphoreType.DMA
    vmem = pl.BlockSpec(memory_space=pltpu.VMEM)
    hbm = pl.BlockSpec(memory_space=pltpu.HBM)
    velocity, density = pl.pallas_call(
        functools.partial(fused_kernel, cells, walls),
        out_shape=(
            pltpu.VMEM((3, columns, own_points), jnp.float32),
            pltpu.VMEM((3, halfway, shard_width), jnp.float32),
        ),
        in_specs=[hbm] * 7,
        out_specs=(vmem, vmem),
        scratch_shapes=[
            pltpu.VMEM((3, columns, own_points), jnp.bfloat16),
            pltpu.VMEM((3, columns, wall_count), jnp.float32),
            pltpu.VMEM((3, halfway, shard_width), jnp.bfloat16),
            pltpu.VMEM((1, columns), jnp.int32),
            pltpu.VMEM((2, cells, walls, 2, halfway, 2 * own_points), jnp.bfloat16),
            pltpu.VMEM((cells, 3, point_count), jnp.float32),
            pltpu.VMEM((walls, 3, wall_count), jnp.float32),
            pltpu.VMEM((walls, 3, wall_count), jnp.float32),
            pltpu.VMEM((walls, 3, halfway, wall_count), jnp.bfloat16),
            pltpu.VMEM((3, wall_count, LANES), jnp.float32),
            pltpu.VMEM((3, point_count, LANES), jnp.float32),
            pltpu.VMEM((cells, 3 * wall_count, 3 * point_count), jnp.bfloat16),
            pltpu.VMEM((walls, 3 * own_points, 3 * wall_count), jnp.bfloat16),
            dma((7,)),
            dma((2, cells - 1)),
            dma((2, cells, walls)),
            dma((2, cells, walls - 1)),
            dma((cells - 1,)),
            dma((cells,)),
            dma((walls - 1, 2)),
            dma((walls, 2)),
            dma((walls - 1,)),
            dma((walls,)),
        ],
        compiler_params=pltpu.CompilerParams(
            collective_id=0, has_side_effects=True, vmem_limit_bytes=VMEM_GRANT
        ),
        name="coupling",
    )(
        mem_pos,
        jnp.transpose(forces, (1, 0, 2)),
        wall_pos,
        wall_normal,
        jnp.transpose(wall_data, (1, 0, 2)),
        jnp.transpose(lag_density, (1, 0, 2)),
        batch_order.reshape(1, columns),
    )
    velocity, density = pl.pallas_call(
        write_kernel,
        out_shape=(
            jax.ShapeDtypeStruct(velocity.shape, velocity.dtype),
            jax.ShapeDtypeStruct(density.shape, density.dtype),
        ),
        in_specs=[vmem] * 2,
        out_specs=(hbm, hbm),
        scratch_shapes=[dma((2,))],
        compiler_params=pltpu.CompilerParams(vmem_limit_bytes=1024 * 1024),
        name="write",
    )(velocity, density)
    return (jnp.transpose(velocity, (1, 0, 2)), jnp.transpose(density, (1, 0, 2)))


VMEM_GRANT = 60 * 1024 * 1024


def step(cells, walls, mem_pos, forces, wall_pos, *rest):
    point_count = mem_pos.shape[1]
    wall_count = wall_pos.shape[1]
    own_points = forces.shape[2]
    shard_width = rest[2].shape[2]
    tiles = 18 * wall_count * (cells * point_count + walls * own_points)
    fits = tiles <= VMEM_GRANT // 2
    aligned = (
        point_count % LANES == 0
        and wall_count % LANES == 0
        and 2 * own_points == LANES
        and 2 * shard_width <= own_points
    )
    if fits and aligned:
        return fused_shards(cells, walls, mem_pos, forces, wall_pos, *rest)
    return shards(mem_pos, forces, wall_pos, *rest)


def solution(mesh):
    placed = (
        P(None, ("groups", "cell")),
        P(None, None, ("groups", "cell", "wall")),
        P(None, ("groups", "wall")),
        P(None, ("groups", "wall")),
        P(None, None, ("groups", "wall")),
        P(None, None, ("groups", "wall", "cell")),
        P(),
    )
    return jax.shard_map(
        functools.partial(step, mesh.shape["cell"], mesh.shape["wall"]),
        mesh=mesh,
        in_specs=placed,
        out_specs=(
            P(None, None, ("groups", "cell", "wall")),
            P(None, None, ("groups", "wall", "cell")),
        ),
        check_vma=False,
    )
```

```python
import functools
import math

import jax
import jax.numpy as jnp
from jax import lax
from jax.experimental import pallas as pl
from jax.experimental.pallas import tpu as pltpu
from jax.sharding import PartitionSpec as P

stokes_coef = 1.0 / (8.0 * math.pi)


def single_tile(targets, sources):
    separation = targets[:, None, :] - sources[:, :, None]
    inverse = lax.rsqrt(jnp.sum(separation * separation, axis=0))
    inverse_cube = inverse * inverse * inverse
    stacked = []
    for second_dim in range(3):
        entries_row = []
        for first_dim in range(3):
            element = separation[first_dim] * separation[second_dim] * inverse_cube
            if first_dim == second_dim:
                element = element + inverse
            entries_row.append(element * stokes_coef)
        stacked.append(jnp.stack(entries_row, axis=1))
    kernel_tile = jnp.stack(stacked, axis=0)
    return kernel_tile.reshape(3 * sources.shape[1], 3 * targets.shape[1]).astype(jnp.bfloat16)


def double_tile(targets, sources, normals):
    separation = targets[:, None, :] - sources[:, :, None]
    inverse = lax.rsqrt(jnp.sum(separation * separation, axis=0))
    normal_flux = jnp.sum(separation * normals[:, :, None], axis=0)
    weight = -6.0 * stokes_coef * normal_flux * inverse**5
    stacked = []
    for second_dim in range(3):
        entries_row = []
        for first_dim in range(3):
            entries_row.append(weight * separation[first_dim] * separation[second_dim])
        stacked.append(jnp.stack(entries_row, axis=1))
    kernel_tile = jnp.stack(stacked, axis=0)
    return kernel_tile.reshape(3 * sources.shape[1], 3 * targets.shape[1]).astype(jnp.bfloat16)


def shards(mem_pos, forces, wall_pos, wall_normal, wall_data, lag_density, batch_order):
    columns = forces.shape[0]
    halfway = columns // 2
    point_count = mem_pos.shape[1]
    wall_count = wall_pos.shape[1]
    shard_width = lag_density.shape[2]
    piece_len = math.gcd(point_count, 128)
    block_count = point_count // piece_len
    first_rows = batch_order[:halfway]
    second_rows = batch_order[halfway:]
    force_block = lax.all_gather(forces, "wall", axis=2, tiled=True)
    lag_block = lax.all_gather(lag_density, "cell", axis=2, tiled=True)
    lag_flat = lag_block.reshape(halfway, 3 * wall_count)

    def position_at(block_index):
        return lax.dynamic_slice_in_dim(mem_pos, block_index * piece_len, piece_len, 1)

    def single_term(block_index):
        loaded = lax.dynamic_slice_in_dim(force_block, block_index * piece_len, piece_len, 2)
        loaded = loaded.reshape(columns, 3 * piece_len)
        return jnp.dot(
            loaded,
            single_tile(wall_pos, position_at(block_index)),
            preferred_element_type=jnp.float32,
        )

    def double_term(dense_rows, block_index):
        kernel_tile = double_tile(position_at(block_index), wall_pos, wall_normal)
        product = jnp.dot(dense_rows, kernel_tile, preferred_element_type=jnp.float32)
        return product.reshape(dense_rows.shape[0], 3, piece_len)

    def place_block(target, piece, block_index):
        return lax.dynamic_update_slice_in_dim(target, piece, block_index * piece_len, 2)

    empty_wall = jnp.zeros((columns, 3 * wall_count), jnp.float32)

    def add_single(block_index, running):
        return running + single_term(block_index)

    running = lax.fori_loop(0, block_count, add_single, empty_wall)
    wall_term = running.reshape(columns, 3, wall_count)
    position_cell = lax.axis_index("cell")
    first_sum = lax.psum(jnp.take(wall_term, first_rows, axis=0), "cell")
    first_block = (2.0 * (jnp.take(wall_data, first_rows, axis=0) - first_sum)).astype(jnp.bfloat16)
    second_sum = lax.psum_scatter(
        jnp.take(wall_term, second_rows, axis=0).astype(jnp.bfloat16),
        "cell",
        scatter_dimension=2,
        tiled=True,
    ).astype(jnp.float32)
    second_data = lax.dynamic_slice_in_dim(
        jnp.take(wall_data, second_rows, axis=0), position_cell * shard_width, shard_width, 2
    )
    wall_density = 2.0 * (second_data - second_sum)
    first_flat = first_block.reshape(halfway, 3 * wall_count)
    carried = jnp.concatenate([lag_flat, first_flat], axis=0)

    def all_terms(block_index, target):
        return place_block(target, double_term(carried, block_index), block_index)

    membrane_term = lax.fori_loop(
        0, block_count, all_terms, jnp.zeros((columns, 3, point_count), jnp.float32)
    )
    batched = lax.psum_scatter(membrane_term, "wall", scatter_dimension=2, tiled=True)
    membrane_velocity = jnp.zeros_like(batched).at[batch_order].set(batched)
    return (membrane_velocity, wall_density)

LANES = 128
MESH = pl.DeviceIdType.MESH
NT = (((1,), (1,)), ((), ()))


def nearest(position, rank, count):
    mirrored = position >= (count + 1) // 2
    here = jnp.where(mirrored, count - 1 - position, position)
    other = jnp.where(rank <= here, rank - 1, rank)
    return jnp.where(mirrored, count - 1 - other, other)


def fused_kernel(
    cells,
    walls,
    mem_hbm,
    force_hbm,
    wall_hbm,
    normal_hbm,
    data_hbm,
    lag_hbm,
    order_hbm,
    out_ref,
    density_ref,
    force_ref,
    data_ref,
    lag_ref,
    order_ref,
    blocks,
    mem_all,
    wall_all,
    first_all,
    wall_cols,
    mem_cols,
    single_all,
    double_all,
    load_sem,
    block_send,
    block_recv,
    forward_send,
    mem_send,
    mem_recv,
    pos_send,
    pos_recv,
    first_send,
    first_recv,
):
    cell = lax.axis_index("cell")
    wall = lax.axis_index("wall")
    columns = order_ref.shape[1]
    halfway = columns // 2
    point_count = mem_hbm.shape[1]
    wall_count = wall_hbm.shape[1]
    own_points = force_ref.shape[2]
    shard_width = lag_ref.shape[2]

    loads = [
        pltpu.make_async_copy(given, held, load_sem.at[at])
        for at, (given, held) in enumerate(
            (
                (order_hbm, order_ref),
                (force_hbm, force_ref),
                (lag_hbm, lag_ref),
                (mem_hbm, mem_all.at[cell]),
                (wall_hbm, wall_all.at[wall, 0]),
                (normal_hbm, wall_all.at[wall, 1]),
                (data_hbm, data_ref),
            )
        )
    ]
    for load in loads:
        load.start()

    cell_peers = [lax.rem(cell + step, cells) for step in range(1, cells)]
    wall_peers = [lax.rem(wall + step, walls) for step in range(1, walls)]

    barrier = pltpu.get_barrier_semaphore()
    for peer in cell_peers:
        pl.semaphore_signal(barrier, inc=1, device_id={"cell": peer}, device_id_type=MESH)
    for peer in wall_peers:
        pl.semaphore_signal(barrier, inc=1, device_id={"wall": peer}, device_id_type=MESH)

    loads[0].wait()
    order_row = order_ref[...]
    row_ids = lax.broadcasted_iota(jnp.int32, (columns, columns), 0)
    col_ids = lax.broadcasted_iota(jnp.int32, (columns, columns), 1)
    scatter = (row_ids == order_row).astype(jnp.float32).astype(jnp.bfloat16)
    unit = (row_ids == col_ids).astype(jnp.float32).astype(jnp.bfloat16)
    gather_f32 = lax.dot_general(unit, scatter, NT, preferred_element_type=jnp.float32)
    gather = gather_f32.astype(jnp.bfloat16)

    loads[1].wait()
    rows = [jnp.dot(gather, force_ref[j], preferred_element_type=jnp.float32) for j in range(3)]
    loads[2].wait()
    lag_rows = [lag_ref[j].astype(jnp.float32) for j in range(3)]
    spare = jnp.zeros((halfway, own_points - 2 * shard_width), jnp.float32)
    unused = jnp.zeros((halfway, own_points - shard_width), jnp.float32)
    halves = (
        ([row[:halfway] for row in rows], (lag_rows[0], lag_rows[1], spare)),
        ([row[halfway:] for row in rows], (lag_rows[2], unused)),
    )
    for wave, (part, rest) in enumerate(halves):
        rest = [piece for piece in rest if piece.shape[1]]
        pair = jnp.concatenate([part[0], part[1]], axis=1)
        blocks[wave, cell, wall, 0] = pair.astype(jnp.bfloat16)
        pair = jnp.concatenate([part[2], *rest], axis=1)
        blocks[wave, cell, wall, 1] = pair.astype(jnp.bfloat16)
    for load in loads[3:6]:
        load.wait()

    def block_copy(wave, source, to_cell, rank):
        return pltpu.make_async_remote_copy(
            blocks.at[wave, source, wall],
            blocks.at[wave, source, wall],
            block_send.at[wave, rank],
            block_recv.at[wave, source, wall],
            device_id={"cell": to_cell},
            device_id_type=MESH,
        )

    def forward_copy(wave, source_cell, source_wall, to_wall, rank, slot):
        return pltpu.make_async_remote_copy(
            blocks.at[wave, source_cell, source_wall],
            blocks.at[wave, source_cell, source_wall],
            forward_send.at[wave, rank, slot],
            block_recv.at[wave, source_cell, source_wall],
            device_id={"wall": to_wall},
            device_id_type=MESH,
        )

    def mem_copy(source, to_cell, rank):
        return pltpu.make_async_remote_copy(
            mem_all.at[source],
            mem_all.at[source],
            mem_send.at[rank],
            mem_recv.at[source],
            device_id={"cell": to_cell},
            device_id_type=MESH,
        )

    def pos_copy(source, to_wall, rank):
        return pltpu.make_async_remote_copy(
            wall_all.at[source],
            wall_all.at[source],
            pos_send.at[rank],
            pos_recv.at[source],
            device_id={"wall": to_wall},
            device_id_type=MESH,
        )

    def first_copy(source, to_wall, rank):
        return pltpu.make_async_remote_copy(
            first_all.at[source],
            first_all.at[source],
            first_send.at[rank],
            first_recv.at[source],
            device_id={"wall": to_wall},
            device_id_type=MESH,
        )

    pl.semaphore_wait(barrier, cells + walls - 2)

    sent = []

    def send(copy):
        sent.append(copy)
        copy.start()

    def send_own(wave):
        for rank in range(cells - 1):
            send(block_copy(wave, cell, nearest(cell, cells - 1 - rank, cells), rank))
        for slot, peer in enumerate(wall_peers):
            send(forward_copy(wave, cell, wall, peer, 0, slot))

    def pass_on(wave, rank):
        source = nearest(cell, rank, cells)
        block_copy(wave, source, source, 0).wait_recv()
        for slot, peer in enumerate(wall_peers):
            send(forward_copy(wave, source, wall, peer, rank, slot))

    send_own(0)
    for rank, peer in enumerate(cell_peers):
        send(mem_copy(cell, peer, rank))
    for rank, peer in enumerate(wall_peers):
        send(pos_copy(wall, peer, rank))
    send_own(1)

    for j in range(3):
        wall_cols[j] = jnp.broadcast_to(wall_all[wall, 0, j : j + 1, :], (LANES, wall_count)).T
        mem_cols[j] = jnp.broadcast_to(mem_all[cell, j : j + 1, :], (LANES, point_count)).T
    loads[6].wait()

    def fill_single(source):
        for start in range(0, point_count, LANES):
            apart = [
                wall_cols[j] - mem_all[source, j : j + 1, start : start + LANES] for j in range(3)
            ]
            square = apart[0] * apart[0] + apart[1] * apart[1] + apart[2] * apart[2]
            inverse = lax.rsqrt(square)
            scaled = stokes_coef * inverse
            cube = scaled * (inverse * inverse)
            for j in range(3):
                along = apart[j] * cube
                for i in range(j + 1):
                    element = along * apart[i]
                    if i == j:
                        element = element + scaled
                    element = element.astype(jnp.bfloat16)
                    for a, b in {(i, j), (j, i)}:
                        single_all[
                            source,
                            a * wall_count : (a + 1) * wall_count,
                            b * point_count + start : b * point_count + start + LANES,
                        ] = element

    def fill_double(source):
        own = pl.ds(pl.multiple_of(wall * own_points, own_points), own_points)
        for start in range(0, wall_count, LANES):
            apart = [
                mem_cols[j, own, :] - wall_all[source, 0, j : j + 1, start : start + LANES]
                for j in range(3)
            ]
            square = apart[0] * apart[0] + apart[1] * apart[1] + apart[2] * apart[2]
            inverse = lax.rsqrt(square)
            flux = (
                apart[0] * wall_all[source, 1, 0:1, start : start + LANES]
                + apart[1] * wall_all[source, 1, 1:2, start : start + LANES]
                + apart[2] * wall_all[source, 1, 2:3, start : start + LANES]
            )
            inverse_square = inverse * inverse
            fifth = inverse_square * inverse_square * inverse
            weight = (-6.0 * stokes_coef) * flux * fifth
            for j in range(3):
                along = apart[j] * weight
                for i in range(j + 1):
                    element = (along * apart[i]).astype(jnp.bfloat16)
                    for a, b in {(i, j), (j, i)}:
                        double_all[
                            source,
                            a * own_points : (a + 1) * own_points,
                            b * wall_count + start : b * wall_count + start + LANES,
                        ] = element

    fill_single(cell)
    fill_double(wall)
    data_rows = [
        jnp.dot(gather_f32, data_ref[j], precision=lax.Precision.HIGHEST) for j in range(3)
    ]

    for rank in range(1, cells):
        pass_on(0, rank)
        source = nearest(cell, rank, cells)
        mem_copy(source, source, 0).wait_recv()
        fill_single(source)
        if rank == 1:
            for peer in wall_peers:
                pos_copy(peer, peer, 0).wait_recv()
                fill_double(peer)
    for rank in range(1, cells):
        pass_on(1, rank)

    def single_layer(wave):
        velocity = jnp.zeros((halfway, 3 * wall_count), jnp.float32)
        for rank in range(cells):
            source = cell if rank == 0 else nearest(cell, rank, cells)
            for peer in wall_peers:
                forward_copy(wave, source, peer, peer, 0, 0).wait_recv()
            pairs = [blocks[wave, source, k, 0] for k in range(walls)]
            thirds = [blocks[wave, source, k, 1] for k in range(walls)]
            loaded = [piece[:, :own_points] for piece in pairs]
            loaded += [piece[:, own_points:] for piece in pairs]
            loaded += [piece[:, :own_points] for piece in thirds]
            velocity = velocity + lax.dot_general(
                jnp.concatenate(loaded, axis=1),
                single_all[source],
                NT,
                preferred_element_type=jnp.float32,
            )
        held = slice(wave * halfway, (wave + 1) * halfway)
        return [
            2.0 * (data_rows[j][held] - velocity[:, j * wall_count : (j + 1) * wall_count])
            for j in range(3)
        ]

    first_rows = single_layer(0)
    for j in range(3):
        first_all[wall, j] = first_rows[j].astype(jnp.bfloat16)
    for rank, peer in enumerate(wall_peers):
        send(first_copy(wall, peer, rank))

    shift = lax.rem((cells - cell) * shard_width, wall_count)
    second_rows = single_layer(1)
    for j in range(3):
        density_ref[j] = pltpu.roll(second_rows[j], shift, 1)[:, :shard_width]

    lag_places = ((0, own_points), (0, own_points + shard_width), (1, own_points))
    total = jnp.zeros((columns, 3 * own_points), jnp.float32)
    for source in range(walls):
        lag = jnp.concatenate(
            [
                blocks[wave, k, source, 1, :, start : start + shard_width]
                for wave, start in lag_places
                for k in range(cells)
            ],
            axis=1,
        )
        placed = jnp.dot(scatter[:, :halfway], lag, preferred_element_type=jnp.float32)
        total = total + lax.dot_general(
            placed.astype(jnp.bfloat16), double_all[source], NT, preferred_element_type=jnp.float32
        )

    last = len(sent) - (walls - 1)
    for copy in sent[:last]:
        copy.wait_send()

    for rank in range(walls):
        source = wall
        if rank:
            source = wall_peers[rank - 1]
            first_copy(source, source, 0).wait_recv()
        first = jnp.concatenate([first_all[source, j] for j in range(3)], axis=1)
        placed = jnp.dot(scatter[:, halfway:], first, preferred_element_type=jnp.float32)
        total = total + lax.dot_general(
            placed.astype(jnp.bfloat16), double_all[source], NT, preferred_element_type=jnp.float32
        )
    for i in range(3):
        out_ref[i] = total[:, i * own_points : (i + 1) * own_points]

    for copy in sent[last:]:
        copy.wait_send()


def write_kernel(velocity_ref, density_ref, velocity_hbm, density_hbm, sem):
    first = pltpu.make_async_copy(velocity_ref, velocity_hbm, sem.at[0])
    second = pltpu.make_async_copy(density_ref, density_hbm, sem.at[1])
    first.start()
    second.start()
    first.wait()
    second.wait()


def fused_shards(cells, walls, mem_pos, forces, wall_pos, wall_normal, wall_data, lag_density, batch_order):
    columns = forces.shape[0]
    halfway = columns // 2
    point_count = mem_pos.shape[1]
    wall_count = wall_pos.shape[1]
    own_points = forces.shape[2]
    shard_width = lag_density.shape[2]
    dma = pltpu.SemaphoreType.DMA
    vmem = pl.BlockSpec(memory_space=pltpu.VMEM)
    hbm = pl.BlockSpec(memory_space=pltpu.HBM)
    velocity, density = pl.pallas_call(
        functools.partial(fused_kernel, cells, walls),
        out_shape=(
            pltpu.VMEM((3, columns, own_points), jnp.float32),
            pltpu.VMEM((3, halfway, shard_width), jnp.float32),
        ),
        in_specs=[hbm] * 7,
        out_specs=(vmem, vmem),
        scratch_shapes=[
            pltpu.VMEM((3, columns, own_points), jnp.bfloat16),
            pltpu.VMEM((3, columns, wall_count), jnp.float32),
            pltpu.VMEM((3, halfway, shard_width), jnp.bfloat16),
            pltpu.VMEM((1, columns), jnp.int32),
            pltpu.VMEM((2, cells, walls, 2, halfway, 2 * own_points), jnp.bfloat16),
            pltpu.VMEM((cells, 3, point_count), jnp.float32),
            pltpu.VMEM((walls, 2, 3, wall_count), jnp.float32),
            pltpu.VMEM((walls, 3, halfway, wall_count), jnp.bfloat16),
            pltpu.VMEM((3, wall_count, LANES), jnp.float32),
            pltpu.VMEM((3, point_count, LANES), jnp.float32),
            pltpu.VMEM((cells, 3 * wall_count, 3 * point_count), jnp.bfloat16),
            pltpu.VMEM((walls, 3 * own_points, 3 * wall_count), jnp.bfloat16),
            dma((7,)),
            dma((2, cells - 1)),
            dma((2, cells, walls)),
            dma((2, cells, walls - 1)),
            dma((cells - 1,)),
            dma((cells,)),
            dma((walls - 1,)),
            dma((walls,)),
            dma((walls - 1,)),
            dma((walls,)),
        ],
        compiler_params=pltpu.CompilerParams(
            collective_id=0, has_side_effects=True, vmem_limit_bytes=VMEM_GRANT
        ),
        name="coupling",
    )(
        mem_pos,
        jnp.transpose(forces, (1, 0, 2)),
        wall_pos,
        wall_normal,
        jnp.transpose(wall_data, (1, 0, 2)),
        jnp.transpose(lag_density, (1, 0, 2)),
        batch_order.reshape(1, columns),
    )
    velocity, density = pl.pallas_call(
        write_kernel,
        out_shape=(
            jax.ShapeDtypeStruct(velocity.shape, velocity.dtype),
            jax.ShapeDtypeStruct(density.shape, density.dtype),
        ),
        in_specs=[vmem] * 2,
        out_specs=(hbm, hbm),
        scratch_shapes=[dma((2,))],
        compiler_params=pltpu.CompilerParams(vmem_limit_bytes=1024 * 1024),
        name="write",
    )(velocity, density)
    return (jnp.transpose(velocity, (1, 0, 2)), jnp.transpose(density, (1, 0, 2)))


VMEM_GRANT = 60 * 1024 * 1024


def step(cells, walls, mem_pos, forces, wall_pos, *rest):
    point_count = mem_pos.shape[1]
    wall_count = wall_pos.shape[1]
    own_points = forces.shape[2]
    shard_width = rest[2].shape[2]
    tiles = 18 * wall_count * (cells * point_count + walls * own_points)
    fits = tiles <= VMEM_GRANT // 2
    aligned = (
        point_count % LANES == 0
        and wall_count % LANES == 0
        and 2 * own_points == LANES
        and 2 * shard_width <= own_points
    )
    if fits and aligned:
        return fused_shards(cells, walls, mem_pos, forces, wall_pos, *rest)
    return shards(mem_pos, forces, wall_pos, *rest)


def solution(mesh):
    placed = (
        P(None, ("groups", "cell")),
        P(None, None, ("groups", "cell", "wall")),
        P(None, ("groups", "wall")),
        P(None, ("groups", "wall")),
        P(None, None, ("groups", "wall")),
        P(None, None, ("groups", "wall", "cell")),
        P(),
    )
    return jax.shard_map(
        functools.partial(step, mesh.shape["cell"], mesh.shape["wall"]),
        mesh=mesh,
        in_specs=placed,
        out_specs=(
            P(None, None, ("groups", "cell", "wall")),
            P(None, None, ("groups", "wall", "cell")),
        ),
        check_vma=False,
    )
```

```python
import functools
import math

import jax
import jax.numpy as jnp
from jax import lax
from jax.experimental import pallas as pl
from jax.experimental.pallas import tpu as pltpu
from jax.sharding import PartitionSpec as P

stokes_coef = 1.0 / (8.0 * math.pi)


def single_tile(targets, sources):
    separation = targets[:, None, :] - sources[:, :, None]
    inverse = lax.rsqrt(jnp.sum(separation * separation, axis=0))
    inverse_cube = inverse * inverse * inverse
    stacked = []
    for second_dim in range(3):
        entries_row = []
        for first_dim in range(3):
            element = separation[first_dim] * separation[second_dim] * inverse_cube
            if first_dim == second_dim:
                element = element + inverse
            entries_row.append(element * stokes_coef)
        stacked.append(jnp.stack(entries_row, axis=1))
    kernel_tile = jnp.stack(stacked, axis=0)
    return kernel_tile.reshape(3 * sources.shape[1], 3 * targets.shape[1]).astype(jnp.bfloat16)


def double_tile(targets, sources, normals):
    separation = targets[:, None, :] - sources[:, :, None]
    inverse = lax.rsqrt(jnp.sum(separation * separation, axis=0))
    normal_flux = jnp.sum(separation * normals[:, :, None], axis=0)
    weight = -6.0 * stokes_coef * normal_flux * inverse**5
    stacked = []
    for second_dim in range(3):
        entries_row = []
        for first_dim in range(3):
            entries_row.append(weight * separation[first_dim] * separation[second_dim])
        stacked.append(jnp.stack(entries_row, axis=1))
    kernel_tile = jnp.stack(stacked, axis=0)
    return kernel_tile.reshape(3 * sources.shape[1], 3 * targets.shape[1]).astype(jnp.bfloat16)


def shards(mem_pos, forces, wall_pos, wall_normal, wall_data, lag_density, batch_order):
    columns = forces.shape[0]
    halfway = columns // 2
    point_count = mem_pos.shape[1]
    wall_count = wall_pos.shape[1]
    shard_width = lag_density.shape[2]
    piece_len = math.gcd(point_count, 128)
    block_count = point_count // piece_len
    first_rows = batch_order[:halfway]
    second_rows = batch_order[halfway:]
    force_block = lax.all_gather(forces, "wall", axis=2, tiled=True)
    lag_block = lax.all_gather(lag_density, "cell", axis=2, tiled=True)
    lag_flat = lag_block.reshape(halfway, 3 * wall_count)

    def position_at(block_index):
        return lax.dynamic_slice_in_dim(mem_pos, block_index * piece_len, piece_len, 1)

    def single_term(block_index):
        loaded = lax.dynamic_slice_in_dim(force_block, block_index * piece_len, piece_len, 2)
        loaded = loaded.reshape(columns, 3 * piece_len)
        return jnp.dot(
            loaded,
            single_tile(wall_pos, position_at(block_index)),
            preferred_element_type=jnp.float32,
        )

    def double_term(dense_rows, block_index):
        kernel_tile = double_tile(position_at(block_index), wall_pos, wall_normal)
        product = jnp.dot(dense_rows, kernel_tile, preferred_element_type=jnp.float32)
        return product.reshape(dense_rows.shape[0], 3, piece_len)

    def place_block(target, piece, block_index):
        return lax.dynamic_update_slice_in_dim(target, piece, block_index * piece_len, 2)

    empty_wall = jnp.zeros((columns, 3 * wall_count), jnp.float32)

    def add_single(block_index, running):
        return running + single_term(block_index)

    running = lax.fori_loop(0, block_count, add_single, empty_wall)
    wall_term = running.reshape(columns, 3, wall_count)
    position_cell = lax.axis_index("cell")
    first_sum = lax.psum(jnp.take(wall_term, first_rows, axis=0), "cell")
    first_block = (2.0 * (jnp.take(wall_data, first_rows, axis=0) - first_sum)).astype(jnp.bfloat16)
    second_sum = lax.psum_scatter(
        jnp.take(wall_term, second_rows, axis=0).astype(jnp.bfloat16),
        "cell",
        scatter_dimension=2,
        tiled=True,
    ).astype(jnp.float32)
    second_data = lax.dynamic_slice_in_dim(
        jnp.take(wall_data, second_rows, axis=0), position_cell * shard_width, shard_width, 2
    )
    wall_density = 2.0 * (second_data - second_sum)
    first_flat = first_block.reshape(halfway, 3 * wall_count)
    carried = jnp.concatenate([lag_flat, first_flat], axis=0)

    def all_terms(block_index, target):
        return place_block(target, double_term(carried, block_index), block_index)

    membrane_term = lax.fori_loop(
        0, block_count, all_terms, jnp.zeros((columns, 3, point_count), jnp.float32)
    )
    batched = lax.psum_scatter(membrane_term, "wall", scatter_dimension=2, tiled=True)
    membrane_velocity = jnp.zeros_like(batched).at[batch_order].set(batched)
    return (membrane_velocity, wall_density)

LANES = 128
MESH = pl.DeviceIdType.MESH
NT = (((1,), (1,)), ((), ()))


def nearest(position, rank, count):
    mirrored = position >= (count + 1) // 2
    here = jnp.where(mirrored, count - 1 - position, position)
    other = jnp.where(rank <= here, rank - 1, rank)
    return jnp.where(mirrored, count - 1 - other, other)


def fused_kernel(
    cells,
    walls,
    mem_hbm,
    force_hbm,
    wall_hbm,
    normal_hbm,
    data_hbm,
    lag_hbm,
    order_hbm,
    out_ref,
    density_ref,
    force_ref,
    data_ref,
    lag_ref,
    order_ref,
    blocks,
    mem_all,
    wall_all,
    first_all,
    wall_cols,
    mem_cols,
    single_all,
    double_all,
    load_sem,
    block_send,
    block_recv,
    forward_send,
    mem_send,
    mem_recv,
    pos_send,
    pos_recv,
    first_send,
    first_recv,
):
    cell = lax.axis_index("cell")
    wall = lax.axis_index("wall")
    columns = order_ref.shape[1]
    halfway = columns // 2
    point_count = mem_hbm.shape[1]
    wall_count = wall_hbm.shape[1]
    own_points = force_ref.shape[2]
    shard_width = lag_ref.shape[2]

    loads = [
        pltpu.make_async_copy(given, held, load_sem.at[at])
        for at, (given, held) in enumerate(
            (
                (order_hbm, order_ref),
                (force_hbm, force_ref),
                (lag_hbm, lag_ref),
                (mem_hbm, mem_all.at[cell]),
                (wall_hbm, wall_all.at[wall, 0]),
                (normal_hbm, wall_all.at[wall, 1]),
                (data_hbm, data_ref),
            )
        )
    ]
    for load in loads:
        load.start()

    cell_peers = [lax.rem(cell + step, cells) for step in range(1, cells)]
    wall_peers = [lax.rem(wall + step, walls) for step in range(1, walls)]

    barrier = pltpu.get_barrier_semaphore()
    for peer in cell_peers:
        pl.semaphore_signal(barrier, inc=1, device_id={"cell": peer}, device_id_type=MESH)
    for peer in wall_peers:
        pl.semaphore_signal(barrier, inc=1, device_id={"wall": peer}, device_id_type=MESH)

    loads[0].wait()
    order_row = order_ref[...]
    row_ids = lax.broadcasted_iota(jnp.int32, (columns, columns), 0)
    col_ids = lax.broadcasted_iota(jnp.int32, (columns, columns), 1)
    scatter = (row_ids == order_row).astype(jnp.float32).astype(jnp.bfloat16)
    unit = (row_ids == col_ids).astype(jnp.float32).astype(jnp.bfloat16)
    gather_f32 = lax.dot_general(unit, scatter, NT, preferred_element_type=jnp.float32)
    gather = gather_f32.astype(jnp.bfloat16)

    loads[1].wait()
    rows = [jnp.dot(gather, force_ref[j], preferred_element_type=jnp.float32) for j in range(3)]
    loads[2].wait()
    lag_rows = [lag_ref[j].astype(jnp.float32) for j in range(3)]
    spare = jnp.zeros((halfway, own_points - 2 * shard_width), jnp.float32)
    unused = jnp.zeros((halfway, own_points - shard_width), jnp.float32)
    halves = (
        ([row[:halfway] for row in rows], (lag_rows[0], lag_rows[1], spare)),
        ([row[halfway:] for row in rows], (lag_rows[2], unused)),
    )
    for wave, (part, rest) in enumerate(halves):
        rest = [piece for piece in rest if piece.shape[1]]
        pair = jnp.concatenate([part[0], part[1]], axis=1)
        blocks[wave, cell, wall, 0] = pair.astype(jnp.bfloat16)
        pair = jnp.concatenate([part[2], *rest], axis=1)
        blocks[wave, cell, wall, 1] = pair.astype(jnp.bfloat16)
    for load in loads[3:6]:
        load.wait()

    def block_copy(wave, source, to_cell, rank):
        return pltpu.make_async_remote_copy(
            blocks.at[wave, source, wall],
            blocks.at[wave, source, wall],
            block_send.at[wave, rank],
            block_recv.at[wave, source, wall],
            device_id={"cell": to_cell},
            device_id_type=MESH,
        )

    def forward_copy(wave, source_cell, source_wall, to_wall, rank, slot):
        return pltpu.make_async_remote_copy(
            blocks.at[wave, source_cell, source_wall],
            blocks.at[wave, source_cell, source_wall],
            forward_send.at[wave, rank, slot],
            block_recv.at[wave, source_cell, source_wall],
            device_id={"wall": to_wall},
            device_id_type=MESH,
        )

    def mem_copy(source, to_cell, rank):
        return pltpu.make_async_remote_copy(
            mem_all.at[source],
            mem_all.at[source],
            mem_send.at[rank],
            mem_recv.at[source],
            device_id={"cell": to_cell},
            device_id_type=MESH,
        )

    def pos_copy(source, to_wall, rank):
        return pltpu.make_async_remote_copy(
            wall_all.at[source],
            wall_all.at[source],
            pos_send.at[rank],
            pos_recv.at[source],
            device_id={"wall": to_wall},
            device_id_type=MESH,
        )

    def first_copy(source, to_wall, rank):
        return pltpu.make_async_remote_copy(
            first_all.at[source],
            first_all.at[source],
            first_send.at[rank],
            first_recv.at[source],
            device_id={"wall": to_wall},
            device_id_type=MESH,
        )

    pl.semaphore_wait(barrier, cells + walls - 2)

    sent = []

    def send(copy):
        sent.append(copy)
        copy.start()

    def send_own(wave):
        for rank in range(cells - 1):
            send(block_copy(wave, cell, nearest(cell, cells - 1 - rank, cells), rank))
        for slot, peer in enumerate(wall_peers):
            send(forward_copy(wave, cell, wall, peer, 0, slot))

    def pass_on(wave, rank):
        source = nearest(cell, rank, cells)
        block_copy(wave, source, source, 0).wait_recv()
        for slot, peer in enumerate(wall_peers):
            send(forward_copy(wave, source, wall, peer, rank, slot))

    send_own(0)
    for rank, peer in enumerate(cell_peers):
        send(mem_copy(cell, peer, rank))
    for rank, peer in enumerate(wall_peers):
        send(pos_copy(wall, peer, rank))
    send_own(1)

    for j in range(3):
        wall_cols[j] = jnp.broadcast_to(wall_all[wall, 0, j : j + 1, :], (LANES, wall_count)).T
        mem_cols[j] = jnp.broadcast_to(mem_all[cell, j : j + 1, :], (LANES, point_count)).T
    loads[6].wait()

    def fill_single(source):
        for start in range(0, point_count, LANES):
            apart = [
                wall_cols[j] - mem_all[source, j : j + 1, start : start + LANES] for j in range(3)
            ]
            square = apart[0] * apart[0] + apart[1] * apart[1] + apart[2] * apart[2]
            inverse = lax.rsqrt(square)
            scaled = stokes_coef * inverse
            cube = scaled * (inverse * inverse)
            for j in range(3):
                along = apart[j] * cube
                for i in range(j + 1):
                    element = along * apart[i]
                    if i == j:
                        element = element + scaled
                    element = element.astype(jnp.bfloat16)
                    for a, b in {(i, j), (j, i)}:
                        single_all[
                            source,
                            a * wall_count : (a + 1) * wall_count,
                            b * point_count + start : b * point_count + start + LANES,
                        ] = element

    def fill_double(source):
        own = pl.ds(pl.multiple_of(wall * own_points, own_points), own_points)
        for start in range(0, wall_count, LANES):
            apart = [
                mem_cols[j, own, :] - wall_all[source, 0, j : j + 1, start : start + LANES]
                for j in range(3)
            ]
            square = apart[0] * apart[0] + apart[1] * apart[1] + apart[2] * apart[2]
            inverse = lax.rsqrt(square)
            flux = (
                apart[0] * wall_all[source, 1, 0:1, start : start + LANES]
                + apart[1] * wall_all[source, 1, 1:2, start : start + LANES]
                + apart[2] * wall_all[source, 1, 2:3, start : start + LANES]
            )
            inverse_square = inverse * inverse
            fifth = inverse_square * inverse_square * inverse
            weight = (-6.0 * stokes_coef) * flux * fifth
            for j in range(3):
                along = apart[j] * weight
                for i in range(j + 1):
                    element = (along * apart[i]).astype(jnp.bfloat16)
                    for a, b in {(i, j), (j, i)}:
                        double_all[
                            source,
                            a * own_points : (a + 1) * own_points,
                            b * wall_count + start : b * wall_count + start + LANES,
                        ] = element

    fill_single(cell)
    fill_double(wall)
    data_rows = [
        jnp.dot(gather_f32, data_ref[j], precision=lax.Precision.HIGHEST) for j in range(3)
    ]

    for rank in range(1, cells):
        pass_on(0, rank)
    for rank in range(1, cells):
        source = nearest(cell, rank, cells)
        mem_copy(source, source, 0).wait_recv()
        fill_single(source)
    for rank in range(1, cells):
        pass_on(1, rank)

    def single_layer(wave):
        velocity = jnp.zeros((halfway, 3 * wall_count), jnp.float32)
        for rank in range(cells):
            source = cell if rank == 0 else nearest(cell, rank, cells)
            for peer in wall_peers:
                forward_copy(wave, source, peer, peer, 0, 0).wait_recv()
            pairs = [blocks[wave, source, k, 0] for k in range(walls)]
            thirds = [blocks[wave, source, k, 1] for k in range(walls)]
            loaded = [piece[:, :own_points] for piece in pairs]
            loaded += [piece[:, own_points:] for piece in pairs]
            loaded += [piece[:, :own_points] for piece in thirds]
            velocity = velocity + lax.dot_general(
                jnp.concatenate(loaded, axis=1),
                single_all[source],
                NT,
                preferred_element_type=jnp.float32,
            )
        held = slice(wave * halfway, (wave + 1) * halfway)
        return [
            2.0 * (data_rows[j][held] - velocity[:, j * wall_count : (j + 1) * wall_count])
            for j in range(3)
        ]

    first_rows = single_layer(0)
    for j in range(3):
        first_all[wall, j] = first_rows[j].astype(jnp.bfloat16)
    for rank, peer in enumerate(wall_peers):
        send(first_copy(wall, peer, rank))

    for peer in wall_peers:
        pos_copy(peer, peer, 0).wait_recv()
        fill_double(peer)
    shift = lax.rem((cells - cell) * shard_width, wall_count)
    second_rows = single_layer(1)
    for j in range(3):
        density_ref[j] = pltpu.roll(second_rows[j], shift, 1)[:, :shard_width]

    lag_places = ((0, own_points), (0, own_points + shard_width), (1, own_points))
    total = jnp.zeros((columns, 3 * own_points), jnp.float32)
    for source in range(walls):
        lag = jnp.concatenate(
            [
                blocks[wave, k, source, 1, :, start : start + shard_width]
                for wave, start in lag_places
                for k in range(cells)
            ],
            axis=1,
        )
        placed = jnp.dot(scatter[:, :halfway], lag, preferred_element_type=jnp.float32)
        total = total + lax.dot_general(
            placed.astype(jnp.bfloat16), double_all[source], NT, preferred_element_type=jnp.float32
        )

    last = len(sent) - (walls - 1)
    for copy in sent[:last]:
        copy.wait_send()

    for rank in range(walls):
        source = wall
        if rank:
            source = wall_peers[rank - 1]
            first_copy(source, source, 0).wait_recv()
        first = jnp.concatenate([first_all[source, j] for j in range(3)], axis=1)
        placed = jnp.dot(scatter[:, halfway:], first, preferred_element_type=jnp.float32)
        total = total + lax.dot_general(
            placed.astype(jnp.bfloat16), double_all[source], NT, preferred_element_type=jnp.float32
        )
    for i in range(3):
        out_ref[i] = total[:, i * own_points : (i + 1) * own_points]

    for copy in sent[last:]:
        copy.wait_send()


def write_kernel(velocity_ref, density_ref, velocity_hbm, density_hbm, sem):
    first = pltpu.make_async_copy(velocity_ref, velocity_hbm, sem.at[0])
    second = pltpu.make_async_copy(density_ref, density_hbm, sem.at[1])
    first.start()
    second.start()
    first.wait()
    second.wait()


def fused_shards(cells, walls, mem_pos, forces, wall_pos, wall_normal, wall_data, lag_density, batch_order):
    columns = forces.shape[0]
    halfway = columns // 2
    point_count = mem_pos.shape[1]
    wall_count = wall_pos.shape[1]
    own_points = forces.shape[2]
    shard_width = lag_density.shape[2]
    dma = pltpu.SemaphoreType.DMA
    vmem = pl.BlockSpec(memory_space=pltpu.VMEM)
    hbm = pl.BlockSpec(memory_space=pltpu.HBM)
    velocity, density = pl.pallas_call(
        functools.partial(fused_kernel, cells, walls),
        out_shape=(
            pltpu.VMEM((3, columns, own_points), jnp.float32),
            pltpu.VMEM((3, halfway, shard_width), jnp.float32),
        ),
        in_specs=[hbm] * 7,
        out_specs=(vmem, vmem),
        scratch_shapes=[
            pltpu.VMEM((3, columns, own_points), jnp.bfloat16),
            pltpu.VMEM((3, columns, wall_count), jnp.float32),
            pltpu.VMEM((3, halfway, shard_width), jnp.bfloat16),
            pltpu.VMEM((1, columns), jnp.int32),
            pltpu.VMEM((2, cells, walls, 2, halfway, 2 * own_points), jnp.bfloat16),
            pltpu.VMEM((cells, 3, point_count), jnp.float32),
            pltpu.VMEM((walls, 2, 3, wall_count), jnp.float32),
            pltpu.VMEM((walls, 3, halfway, wall_count), jnp.bfloat16),
            pltpu.VMEM((3, wall_count, LANES), jnp.float32),
            pltpu.VMEM((3, point_count, LANES), jnp.float32),
            pltpu.VMEM((cells, 3 * wall_count, 3 * point_count), jnp.bfloat16),
            pltpu.VMEM((walls, 3 * own_points, 3 * wall_count), jnp.bfloat16),
            dma((7,)),
            dma((2, cells - 1)),
            dma((2, cells, walls)),
            dma((2, cells, walls - 1)),
            dma((cells - 1,)),
            dma((cells,)),
            dma((walls - 1,)),
            dma((walls,)),
            dma((walls - 1,)),
            dma((walls,)),
        ],
        compiler_params=pltpu.CompilerParams(
            collective_id=0, has_side_effects=True, vmem_limit_bytes=VMEM_GRANT
        ),
        name="coupling",
    )(
        mem_pos,
        jnp.transpose(forces, (1, 0, 2)),
        wall_pos,
        wall_normal,
        jnp.transpose(wall_data, (1, 0, 2)),
        jnp.transpose(lag_density, (1, 0, 2)),
        batch_order.reshape(1, columns),
    )
    velocity, density = pl.pallas_call(
        write_kernel,
        out_shape=(
            jax.ShapeDtypeStruct(velocity.shape, velocity.dtype),
            jax.ShapeDtypeStruct(density.shape, density.dtype),
        ),
        in_specs=[vmem] * 2,
        out_specs=(hbm, hbm),
        scratch_shapes=[dma((2,))],
        compiler_params=pltpu.CompilerParams(vmem_limit_bytes=1024 * 1024),
        name="write",
    )(velocity, density)
    return (jnp.transpose(velocity, (1, 0, 2)), jnp.transpose(density, (1, 0, 2)))


VMEM_GRANT = 60 * 1024 * 1024


def step(cells, walls, mem_pos, forces, wall_pos, *rest):
    point_count = mem_pos.shape[1]
    wall_count = wall_pos.shape[1]
    own_points = forces.shape[2]
    shard_width = rest[2].shape[2]
    tiles = 18 * wall_count * (cells * point_count + walls * own_points)
    fits = tiles <= VMEM_GRANT // 2
    aligned = (
        point_count % LANES == 0
        and wall_count % LANES == 0
        and 2 * own_points == LANES
        and 2 * shard_width <= own_points
    )
    if fits and aligned:
        return fused_shards(cells, walls, mem_pos, forces, wall_pos, *rest)
    return shards(mem_pos, forces, wall_pos, *rest)


def solution(mesh):
    placed = (
        P(None, ("groups", "cell")),
        P(None, None, ("groups", "cell", "wall")),
        P(None, ("groups", "wall")),
        P(None, ("groups", "wall")),
        P(None, None, ("groups", "wall")),
        P(None, None, ("groups", "wall", "cell")),
        P(),
    )
    return jax.shard_map(
        functools.partial(step, mesh.shape["cell"], mesh.shape["wall"]),
        mesh=mesh,
        in_specs=placed,
        out_specs=(
            P(None, None, ("groups", "cell", "wall")),
            P(None, None, ("groups", "wall", "cell")),
        ),
        check_vma=False,
    )
```
